256 devices in a mesh: seq: 32 (over x, z), head: 8 (over y, core).
Axes of the slice: x: 4, y: 4, z: 8, core: 2. Of those that a mesh axis runs over, the one named last changes fastest.
Arguments:
- queries: bfloat16 [4, 256, 64, 128], P(None, 'seq', 'head')
- new_kv: bfloat16 [2, 4, 256, 8, 128], P(None, None, 'seq', 'head'), may hold values from -12 to 12
- prompt_keys: bfloat16 [8, 32768, 8, 128], P(None, 'seq', 'head')
- prompt_values: bfloat16 [8, 32768, 8, 128], P(None, 'seq', 'head'), may hold values from -6 to 6
- suffix_kv: bfloat16 [2, 256, 512, 8, 128], P(None, 'seq', None, 'head'), may hold values from -9.5625 to 9.5625
- prompt_ids: int32 [256, 1], P('seq'), may hold values from 0 to 7
- suffix_lengths: int32 [256], P('seq'), may hold values from 1 to 512, 65536 in all
- token_ids: int32 [256, 4], replicated, may hold values from 0 to 65535
- embedding: bfloat16 [65536, 8192], P('head', 'seq'), may hold values from -3 to 3
- out_weight: bfloat16 [8192, 8192], P('head', 'seq'), may hold values from -0.25 to 0.25
Outputs:
- hidden_out: bfloat16 [256, 4, 8192], P('head', None, 'seq')
The draws below stay inside these ranges and needn't reach their ends.
Inputs may be any that keep to these rules, and one draw needn't show every extreme that they name: `prompt_ids`: every one of the 8 prompts is named by some row.
All inputs are finite; a program needn't handle non-finite values. No bound on the sum of `suffix_lengths` on one device may be relied on, other than what follows from the above.
Results may differ from the reference program's by a relative error of at most 0.02.
Values may be sent and summed in bfloat16 or wider, within the bound.
No kernel may reach another device: no remote copies, remote signals or barrier semaphores. Data moves between devices by JAX's collectives and lax.ppermute only.
A program may use at most 320 MiB of HBM per device.

```python
import math
import jax
import jax.numpy as jnp
import numpy as np
from jax import lax

D = 8192
H = 64
KVH = 8
HD = 128
VOCAB = 65536
STEPS = 4
PROMPTS = 8
SUF = 512
ROWS = 256
PLEN = 32768


def draw_queries(key, part):
    values = 2.5 * jax.random.normal(jax.random.fold_in(key, 11), (STEPS, ROWS, H, HD), jnp.float32)
    values = jnp.clip(values, -15.0, 15.0)
    return values.astype(jnp.bfloat16)


def draw_prompt_keys(key, part):
    values = jax.random.normal(jax.random.fold_in(key, 12), (PROMPTS, PLEN, KVH, HD), jnp.float32)
    values = jnp.clip(values, -6.0, 6.0)
    return values.astype(jnp.bfloat16)


def place_ends(array, own_key, low, high):
    dims = array.shape
    index_at = [jax.random.randint(jax.random.fold_in(own_key, axis), (), 0, dims[axis]) for axis in range(len(dims))]
    array = array.at[tuple(index_at)].set(low)
    longest = dims.index(max(dims))
    index_at[longest] = (index_at[longest] + 1) % dims[longest]
    return array.at[tuple(index_at)].set(high)


def levels(stream_key, extent, cuts, least, largest):
    def one(dim, shards_of):
        draws = jax.random.uniform(jax.random.fold_in(jax.random.fold_in(stream_key, 6), dim), (shards_of,), jnp.float32, least / len(cuts), largest / len(cuts))
        return jnp.repeat(jnp.exp(draws), extent[dim] // shards_of).reshape((-1,) + (1,) * (len(extent) - dim - 1))

    gain = one(*cuts[0])
    for cut in cuts[1:]:
        gain = gain * one(*cut)
    return gain


def rank_table(number_of, lean):
    weights = [(1 << 20) // math.isqrt(grade ** lean) + 1 for grade in range(1, number_of + 1)]
    scale = 1 + sum(weights) // (1 << 30)
    return np.cumsum(np.array([max(1, weight // scale) for weight in weights]))


def ranked_ids(key, extent, count, lean):
    grid = rank_table(count, lean)
    pick = jax.random.randint(jax.random.fold_in(key, 1), extent, 0, int(grid[count - 1]))
    standing = jnp.searchsorted(jnp.asarray(grid, jnp.int32), pick, side="right")
    return jax.random.permutation(jax.random.fold_in(key, 2), count)[standing].astype(jnp.int32)


def different_ones(own_key, rows, number_of, top, lift):
    ranking = jax.random.permutation(jax.random.fold_in(own_key, 1), number_of)
    favour = ranking
    for power in range(3):
        favour = favour * favour // number_of
    favour = favour * lift // number_of
    chance = jax.random.randint(jax.random.fold_in(own_key, 2), (rows, number_of), 0, 4096) + favour
    holders = jax.random.permutation(jax.random.fold_in(own_key, 3), rows)[jnp.arange(number_of) % rows]
    chance = jnp.where(jnp.arange(rows)[:, None] == holders[None, :], 1 << 14, chance)
    merit = chance * number_of + jnp.arange(number_of)
    return lax.top_k(merit.astype(jnp.int32), top)[1].astype(jnp.int32)


def length_profile(amount, total, most, lean):
    weights = [(1 << 20) // math.isqrt(grade ** lean) + 1 for grade in range(2, amount + 1)]
    spare, holding = total - most - (amount - 1), [1] * (amount - 1)
    while spare > 0:
        candidates = [i for i in range(amount - 1) if holding[i] < most]
        pool, left = sum([weights[i] for i in candidates]), spare
        for i in candidates:
            extra = min(most - holding[i], max(1, left * weights[i] // pool), spare)
            holding[i] = holding[i] + extra
            spare = spare - extra
    return np.array([most] + holding)


def uneven_parts(key, count, total, limit, slope):
    if count == 2:
        one = jax.random.randint(key, (), max(1, total - limit), min(limit, total - 1) + 1)
        return jnp.stack([one, total - one])
    lengths = jnp.asarray(length_profile(count, total, limit, slope), jnp.int32)
    pairs = (count - 1) // 2
    source_of, sink = lengths[1:1 + 2 * pairs:2], lengths[2:2 + 2 * pairs:2]
    slack = jnp.minimum(source_of - 1, limit - sink)
    shifted = jax.random.randint(jax.random.fold_in(key, 1), (pairs,), 0, 1 << 20) % (slack + 1)
    lengths = lengths.at[1:1 + 2 * pairs:2].set(source_of - shifted).at[2:2 + 2 * pairs:2].set(sink + shifted)
    return lengths[jax.random.permutation(jax.random.fold_in(key, 2), count)]


def bell_draw(rng, extent, deviation, most, cuts=(), held_as=jnp.bfloat16):
    values = deviation * jax.random.normal(rng, extent, jnp.float32)
    if cuts:
        values = values * levels(rng, extent, cuts, -0.22, 0.18)
    return jnp.clip(values, -most, most).astype(held_as)


def setup_inputs(seed: int = 0) -> dict:
    keys = jax.random.split(jax.random.key(seed), 11)
    return {
        "queries": draw_queries(jax.random.fold_in(keys[10], 71), 0),
        "new_kv": bell_draw(keys[1], (2, STEPS, ROWS, KVH, HD), 2.0, 12.0, ((2, 32), (3, 8))),
        "prompt_keys": draw_prompt_keys(jax.random.fold_in(keys[10], 71), 0),
        "prompt_values": bell_draw(keys[3], (PROMPTS, PLEN, KVH, HD), 1.0, 6.0, ((1, 32), (2, 8))),
        "suffix_kv": bell_draw(keys[4], (2, ROWS, SUF, KVH, HD), 1.6, 9.5625, ((1, 32), (3, 8))),
        "prompt_ids": different_ones(keys[5], ROWS, PROMPTS, 1, 1024),
        "suffix_lengths": uneven_parts(keys[6], ROWS, ROWS * SUF // 2, SUF, 2).astype(jnp.int32),
        "token_ids": place_ends(ranked_ids(keys[7], (ROWS, STEPS), VOCAB, 2), jax.random.fold_in(keys[7], 3), 0, VOCAB - 1).astype(jnp.int32),
        "embedding": bell_draw(keys[8], (VOCAB, D), 0.5, 3.0, ((0, 8), (1, 32))),
        "out_weight": bell_draw(keys[9], (H * HD, D), (4 * HD) ** -0.5, 0.25, ((0, 8), (1, 32))),
    }


def rounded(weights):
    return lax.optimization_barrier(weights.astype(jnp.bfloat16)).astype(jnp.float32)


def reference(queries, new_kv, prompt_keys, prompt_values, suffix_kv, prompt_ids, suffix_lengths, token_ids, embedding, out_weight):
    group_size = H // KVH
    score_scale = HD ** -0.5
    live_pos = jnp.arange(SUF, dtype=jnp.int32)
    step_order = jnp.arange(STEPS, dtype=jnp.int32)
    causal = step_order[None, :] <= step_order[:, None]
    row_queries = jnp.moveaxis(queries, 1, 0)
    row_fresh = jnp.moveaxis(new_kv, 2, 0)
    row_suffix = jnp.moveaxis(suffix_kv, 1, 0)

    def one_row(inputs):
        query_rows, fresh_rows, suffix, prompt_row, length = inputs
        query_f = query_rows.astype(jnp.float32).reshape(STEPS, KVH, group_size, HD)
        prompt_key = prompt_keys[prompt_row].astype(jnp.float32)
        prompt_val = prompt_values[prompt_row].astype(jnp.float32)
        score_prompt = jnp.einsum("tcgd,kcd->ctgk", query_f, prompt_key) * score_scale
        score_suffix = jnp.einsum("tcgd,kcd->ctgk", query_f, suffix[0].astype(jnp.float32)) * score_scale
        live_mask = (live_pos < length)[None, None, None, :]
        score_suffix = jnp.where(live_mask, score_suffix, -jnp.inf)
        score_fresh = jnp.einsum("tcgd,ucd->ctgu", query_f, fresh_rows[0].astype(jnp.float32)) * score_scale
        score_fresh = jnp.where(causal[None, :, None, :], score_fresh, -jnp.inf)
        highest = jnp.maximum(jnp.max(score_prompt, axis=-1), jnp.maximum(jnp.max(score_suffix, axis=-1), jnp.max(score_fresh, axis=-1)))
        weight_prompt = jnp.exp(score_prompt - highest[..., None])
        weight_suffix = jnp.exp(score_suffix - highest[..., None])
        weight_fresh = jnp.exp(score_fresh - highest[..., None])
        denominator = jnp.sum(weight_prompt, axis=-1) + jnp.sum(weight_suffix, axis=-1) + jnp.sum(weight_fresh, axis=-1)
        blended = jnp.einsum("ctgk,kcd->ctgd", rounded(weight_prompt), prompt_val)
        blended = blended + jnp.einsum("ctgk,kcd->ctgd", rounded(weight_suffix), suffix[1].astype(jnp.float32))
        blended = blended + jnp.einsum("ctgu,ucd->ctgd", rounded(weight_fresh), fresh_rows[1].astype(jnp.float32))
        return (blended / denominator[..., None]).astype(jnp.bfloat16)

    attention = lax.map(one_row, (row_queries, row_fresh, row_suffix, prompt_ids[:, 0].astype(jnp.int32), suffix_lengths.astype(jnp.int32)))
    weight_full = out_weight.astype(jnp.float32).reshape(KVH, group_size, HD, D)
    projected = jnp.einsum("rctgd,cgde->rte", attention.astype(jnp.float32), weight_full)
    embedded = jnp.take(embedding, token_ids, axis=0).astype(jnp.float32)
    return (projected + embedded).astype(jnp.bfloat16)
```

```python
import functools
import math

import jax
import jax.numpy as jnp
from jax import lax
from jax.experimental import pallas as pl
from jax.experimental.pallas import tpu as pltpu
from jax.sharding import PartitionSpec as P

BLOCK_ROWS = 8
PACK = 16
LOG2E = 1.0 / math.log(2.0)
SEQ_X, SEQ_Z = 4, 8
Z_GROUPS = [[x * SEQ_Z + z for z in range(SEQ_Z)] for x in range(SEQ_X)]
X_GROUPS = [[x * SEQ_Z + z for x in range(SEQ_X)] for z in range(SEQ_Z)]
VMEM = pl.BlockSpec(memory_space=pltpu.VMEM)
SMEM = pl.BlockSpec(memory_space=pltpu.SMEM)


def three_terms(x):
    hi = x.astype(jnp.bfloat16).astype(jnp.float32)
    mid = (x - hi).astype(jnp.bfloat16).astype(jnp.float32)
    return hi, mid, (x - hi) - mid


def prompt_kernel(per_row, scale, slot_ref, count_ref, q_ref, k_ref, v_ref, out_ref, stat_ref):
    owners = out_ref.shape[0]
    queries = BLOCK_ROWS * per_row
    body_rows = BLOCK_ROWS * per_row

    def block(b, carry):
        rows = []
        for j in range(BLOCK_ROWS):
            rows.append(slot_ref[b * BLOCK_ROWS + j] // 8)
        prompt = slot_ref[b * BLOCK_ROWS] % 8
        where = [(r // 8, pl.ds(pl.multiple_of((r % 8) * per_row, per_row), per_row)) for r in rows]
        q = jnp.concatenate([q_ref[o, w, :] for o, w in where], axis=0)
        s = lax.dot_general(
            q, k_ref[prompt], (((1,), (1,)), ((), ())), preferred_element_type=jnp.float32
        )
        top = jnp.max(s, axis=-1, keepdims=True) * scale
        p = jnp.exp2(s * scale - top)
        total = jnp.sum(p, axis=-1, keepdims=True)
        mixed = jnp.dot(
            p.astype(jnp.bfloat16), v_ref[prompt], preferred_element_type=jnp.float32
        )
        mixed = (mixed / total).astype(jnp.bfloat16)
        hi, mid, lo = three_terms(top)
        lane = lax.broadcasted_iota(jnp.int32, (queries, 128), 1)
        at = lax.broadcasted_iota(jnp.int32, (queries, 128), 0) % per_row
        part = lane // per_row
        stat = jnp.where(part == 0, hi, jnp.where(part == 1, mid, jnp.where(part == 2, lo, total)))
        stat = jnp.where(lane % per_row == at, stat, 0.0)
        stat = jnp.sum(stat.reshape(BLOCK_ROWS, per_row, 128), axis=1)
        for j in range(BLOCK_ROWS):
            o, w = where[j]
            out_ref[o, w, :] = mixed[j * per_row : (j + 1) * per_row, :]
            stat_ref[pl.ds(rows[j], 1), :] = stat[j : j + 1, :]
        return carry

    lax.fori_loop(0, count_ref[0], block, 0)
    for o in range(owners):
        stats = jnp.concatenate(
            [stat_ref[o * 8 : (o + 1) * 8, :], jnp.zeros((PACK - 8, 128), jnp.float32)], axis=0
        )
        out_ref[o, body_rows : body_rows + PACK, :] = stats.astype(jnp.bfloat16)


def own_kernel(per_row, steps, scale, len_ref, q_ref, kv_ref, fresh_ref, out_ref, top_ref, total_ref):
    rows, length = kv_ref.shape[1], kv_ref.shape[2]
    group = per_row // steps
    pos = lax.broadcasted_iota(jnp.int32, (per_row, length), 1)
    step_of = lax.broadcasted_iota(jnp.int32, (per_row, PACK), 0) // group
    fresh_at = lax.broadcasted_iota(jnp.int32, (per_row, PACK), 1)
    over_last = (((1,), (1,)), ((), ()))
    for j in range(rows):
        part = pl.ds(j * per_row, per_row)
        q = q_ref[part, :]
        s = lax.dot_general(q, kv_ref[0, j], over_last, preferred_element_type=jnp.float32)
        s = jnp.where(pos < len_ref[j], s * scale, -jnp.inf)
        f = lax.dot_general(q, fresh_ref[0, j], over_last, preferred_element_type=jnp.float32)
        f = jnp.where(fresh_at <= step_of, f * scale, -jnp.inf)
        top = jnp.maximum(
            jnp.max(s, axis=-1, keepdims=True), jnp.max(f, axis=-1, keepdims=True)
        )
        ps, pf = jnp.exp2(s - top), jnp.exp2(f - top)
        total = jnp.sum(ps, axis=-1, keepdims=True) + jnp.sum(pf, axis=-1, keepdims=True)
        mixed = jnp.dot(ps.astype(jnp.bfloat16), kv_ref[1, j], preferred_element_type=jnp.float32)
        mixed += jnp.dot(
            pf.astype(jnp.bfloat16), fresh_ref[1, j], preferred_element_type=jnp.float32
        )
        out_ref[part, :] = mixed
        top_ref[part, :] = jnp.broadcast_to(top, (per_row, 128))
        total_ref[part, :] = jnp.broadcast_to(total, (per_row, 128))


def merge_kernel(per_row, parts_ref, own_ref, top_ref, total_ref, out_ref):
    sources = parts_ref.shape[0]
    rows = 8
    stat = parts_ref[:, rows * per_row : rows * per_row + PACK, :].astype(jnp.float32)[:, :rows, :]
    stat = stat.reshape(sources * rows, 128)
    top = (
        stat
        + pltpu.roll(stat, 128 - per_row, 1)
        + pltpu.roll(stat, 128 - 2 * per_row, 1)
    )
    total = pltpu.roll(stat, 128 - 3 * per_row, 1)
    top = top.reshape(sources, rows, 128)
    total = total.reshape(sources, rows, 128)
    peak = jnp.max(top, axis=0)
    weight = total * jnp.exp2(top - peak[None])
    summed = jnp.sum(weight, axis=0)
    for j in range(rows):
        table = jnp.concatenate(
            [weight[:, j, :], peak[j : j + 1, :], summed[j : j + 1, :], jnp.zeros((6, 128), jnp.float32)],
            axis=0,
        )
        table = jnp.transpose(table)[:per_row, :]
        span = slice(j * per_row, (j + 1) * per_row)
        acc = jnp.zeros((per_row, 128), jnp.float32)
        for i in range(sources):
            acc += table[:, i : i + 1] * parts_ref[i, span, :].astype(jnp.float32)
        prompt_top = table[:, sources : sources + 1]
        prompt_sum = table[:, sources + 1 : sources + 2]
        own_top = top_ref[span, :]
        best = jnp.maximum(prompt_top, own_top)
        a, b = jnp.exp2(prompt_top - best), jnp.exp2(own_top - best)
        num = acc * a + own_ref[span, :] * b
        den = prompt_sum * a + total_ref[span, :] * b
        out_ref[span, :] = (num / den).astype(jnp.bfloat16)


def slots(ids, prompts):
    rows = ids.shape[0]
    blocks = rows // BLOCK_ROWS + prompts
    r = jnp.arange(rows, dtype=jnp.int32)
    p = jnp.arange(prompts, dtype=jnp.int32)
    named = ids[None, :] == p[:, None]
    need = (jnp.sum(named.astype(jnp.int32), axis=1) + BLOCK_ROWS - 1) // BLOCK_ROWS
    first = jnp.sum(jnp.where(p[None, :] < p[:, None], need[None, :], 0), axis=1) * BLOCK_ROWS
    before = jnp.sum(
        ((ids[None, :] == ids[:, None]) & (r[None, :] < r[:, None])).astype(jnp.int32), axis=1
    )
    place = jnp.sum(jnp.where(named, first[:, None], 0), axis=0) + before
    code = (place * rows + r) * 8 + ids
    k = jnp.arange(blocks * BLOCK_ROWS, dtype=jnp.int32)
    best = jnp.max(jnp.where(place[None, :] <= k[:, None], code[None, :], 0), axis=1)
    return best % (rows * 8), jnp.sum(need).reshape(1)


def spread(x, groups):
    n = len(groups[0])
    return lax.all_to_all(
        jnp.broadcast_to(x[None], (n,) + x.shape), "seq", 0, 0, axis_index_groups=groups
    )


def gather_seq(x):
    zs = spread(x, Z_GROUPS)
    xs = spread(zs, X_GROUPS)
    return xs.reshape((SEQ_X * SEQ_Z,) + x.shape)


def shards(
    queries,
    new_kv,
    prompt_keys,
    prompt_values,
    suffix_kv,
    prompt_ids,
    suffix_lengths,
    token_ids,
    embedding,
    out_weight,
):
    steps, rows_own, heads_own, head_dim = queries.shape
    prompts, positions = prompt_keys.shape[0], prompt_keys.shape[1]
    per_row = steps * heads_own
    scale = head_dim ** (-0.5) * LOG2E
    own_q = jnp.transpose(queries, (1, 0, 2, 3)).reshape(rows_own * per_row, head_dim)
    id_rows = jnp.broadcast_to(prompt_ids.astype(jnp.bfloat16), (rows_own, head_dim))
    packed = jnp.concatenate([own_q, id_rows, jnp.zeros((PACK - rows_own, head_dim), jnp.bfloat16)])
    all_q = gather_seq(packed)
    sources = all_q.shape[0]
    ids = all_q[:, rows_own * per_row : rows_own * per_row + rows_own, 0].reshape(-1)
    slot, count = slots(ids.astype(jnp.int32), prompts)

    payload = jax.ShapeDtypeStruct((sources, rows_own * per_row + PACK, head_dim), jnp.bfloat16)
    partial = pl.pallas_call(
        functools.partial(prompt_kernel, per_row, scale),
        out_shape=payload,
        in_specs=[SMEM, SMEM, VMEM, VMEM, VMEM],
        out_specs=VMEM,
        scratch_shapes=[pltpu.VMEM((sources * rows_own, 128), jnp.float32)],
        compiler_params=pltpu.CompilerParams(vmem_limit_bytes=48 << 20),
        name="prompt",
    )(
        slot,
        count,
        all_q,
        prompt_keys.reshape(prompts, positions, head_dim),
        prompt_values.reshape(prompts, positions, head_dim),
    )

    fresh = jnp.transpose(new_kv[:, :, :, 0, :], (0, 2, 1, 3))
    fresh = jnp.pad(fresh, ((0, 0), (0, 0), (0, PACK - steps), (0, 0)))
    wide = jax.ShapeDtypeStruct((rows_own * per_row, head_dim), jnp.float32)
    own = pl.pallas_call(
        functools.partial(own_kernel, per_row, steps, scale),
        out_shape=[wide, wide, wide],
        in_specs=[SMEM, VMEM, VMEM, VMEM],
        out_specs=[VMEM] * 3,
        compiler_params=pltpu.CompilerParams(vmem_limit_bytes=32 << 20),
        name="own",
    )(suffix_lengths, own_q, suffix_kv[:, :, :, 0, :], fresh)

    received = lax.all_to_all(partial, "seq", 0, 0)
    attention = pl.pallas_call(
        functools.partial(merge_kernel, per_row),
        out_shape=jax.ShapeDtypeStruct((rows_own * per_row, head_dim), jnp.bfloat16),
        in_specs=[VMEM] * 4,
        out_specs=VMEM,
        compiler_params=pltpu.CompilerParams(vmem_limit_bytes=32 << 20),
        name="merge",
    )(received, *own)
    attention = attention.reshape(rows_own * steps, heads_own * head_dim)
    attention_all = gather_seq(attention).reshape(-1, heads_own * head_dim)

    vocab_own = embedding.shape[0]
    local_ids = token_ids.reshape(-1) - lax.axis_index("head") * vocab_own
    inside = (local_ids >= 0) & (local_ids < vocab_own)
    embedded = jnp.take(embedding, jnp.clip(local_ids, 0, vocab_own - 1), axis=0)
    embedded = jnp.where(inside[:, None], embedded.astype(jnp.float32), 0.0)
    projected = jnp.dot(attention_all, out_weight, preferred_element_type=jnp.float32)
    terms = (projected + embedded).astype(jnp.bfloat16)
    heads = lax.axis_size("head")
    terms = lax.all_to_all(terms.reshape(heads, -1, terms.shape[1]), "head", 0, 0)
    hidden = jnp.sum(terms.astype(jnp.float32), axis=0).astype(jnp.bfloat16)
    return hidden.reshape(-1, steps, hidden.shape[1])


def solution(mesh):
    return jax.shard_map(
        shards,
        mesh=mesh,
        in_specs=(
            P(None, "seq", "head", None),
            P(None, None, "seq", "head", None),
            P(None, "seq", "head", None),
            P(None, "seq", "head", None),
            P(None, "seq", None, "head", None),
            P("seq", None),
            P("seq"),
            P(),
            P("head", "seq"),
            P("head", "seq"),
        ),
        out_specs=P("head", None, "seq"),
        check_vma=False,
    )
```

```python
import functools
import math

import jax
import jax.numpy as jnp
from jax import lax
from jax.experimental import pallas as pl
from jax.experimental.pallas import tpu as pltpu
from jax.sharding import PartitionSpec as P

BLOCK_ROWS = 4
DEPTH = 2
OWNER_ROWS = 8
PACK = 16
LOG2E = 1.0 / math.log(2.0)
SEQ_X, SEQ_Z = 4, 8
Z_GROUPS = [[x * SEQ_Z + z for z in range(SEQ_Z)] for x in range(SEQ_X)]
X_GROUPS = [[x * SEQ_Z + z for x in range(SEQ_X)] for z in range(SEQ_Z)]
VMEM = pl.BlockSpec(memory_space=pltpu.VMEM)
SMEM = pl.BlockSpec(memory_space=pltpu.SMEM)
HBM = pl.BlockSpec(memory_space=pltpu.HBM)


def three_terms(x):
    hi = x.astype(jnp.bfloat16).astype(jnp.float32)
    mid = (x - hi).astype(jnp.bfloat16).astype(jnp.float32)
    return hi, mid, (x - hi) - mid


def in_hbm(x):
    return pltpu.with_memory_space_constraint(x, pltpu.HBM)


def slot_table(rows, prompts, ids_ref, slot_ref, next_ref):
    for p in range(prompts):
        next_ref[p] = 0

    def count(r, carry):
        p = ids_ref[r // OWNER_ROWS, r % OWNER_ROWS]
        next_ref[p] = next_ref[p] + 1
        return carry

    def place(r, carry):
        p = ids_ref[r // OWNER_ROWS, r % OWNER_ROWS]
        k = next_ref[p]
        slot_ref[k] = r * prompts + p
        next_ref[p] = k + 1
        return carry

    lax.fori_loop(0, rows, count, 0, unroll=True)
    end = jnp.int32(0)
    ends = []
    for p in range(prompts):
        need = (next_ref[p] + BLOCK_ROWS - 1) // BLOCK_ROWS * BLOCK_ROWS
        next_ref[p] = end
        end = end + need
        ends.append(end)
    lax.fori_loop(0, rows, place, 0, unroll=True)
    for p in range(prompts):
        filled = next_ref[p]
        last = slot_ref[jnp.maximum(filled - 1, 0)]
        for i in range(BLOCK_ROWS - 1):

            @pl.when(filled + i < ends[p])
            def _():
                slot_ref[filled + i] = last

    return end // BLOCK_ROWS


def prompt_kernel(
    per_row,
    scale,
    q_ref,
    k_hbm,
    v_hbm,
    out_ref,
    k_ref,
    v_ref,
    stat_ref,
    score_ref,
    slot_ref,
    next_ref,
    held_ref,
    ids_ref,
    ids_sem,
    k_sem,
    v_sem,
):
    owners = out_ref.shape[0]
    prompts = k_ref.shape[0]
    queries = BLOCK_ROWS * per_row
    body_rows = OWNER_ROWS * per_row
    def load(p):
        return (
            pltpu.make_async_copy(k_hbm.at[p], k_ref.at[p], k_sem.at[p]),
            pltpu.make_async_copy(v_hbm.at[p], v_ref.at[p], v_sem.at[p]),
        )

    def finish(p, carry):
        for copy in load(p):
            copy.wait()
        return carry

    held_ref[...] = q_ref[:, body_rows, :].astype(jnp.float32).astype(jnp.int32)
    ids_copy = pltpu.make_async_copy(held_ref, ids_ref, ids_sem)
    ids_copy.start()
    for p in range(prompts):
        for copy in load(p):
            copy.start()
    ids_copy.wait()
    blocks = slot_table(owners * OWNER_ROWS, prompts, ids_ref, slot_ref, next_ref)

    def locate(b):
        codes = [slot_ref[b * BLOCK_ROWS + j] for j in range(BLOCK_ROWS)]
        rows = [code // prompts for code in codes]
        where = [
            (r // OWNER_ROWS, pl.ds(pl.multiple_of(r % OWNER_ROWS * per_row, per_row), per_row))
            for r in rows
        ]
        return rows, where, codes[0] % prompts

    def score(b, at):
        _, where, prompt = locate(b)
        q = jnp.concatenate([q_ref[o, w, :] for o, w in where], axis=0)
        score_ref[at] = lax.dot_general(
            q, k_ref[prompt], (((1,), (1,)), ((), ())), preferred_element_type=jnp.float32
        )

    def mix(b, at):
        rows, where, prompt = locate(b)
        s = score_ref[at]
        top = jnp.max(s, axis=-1, keepdims=True) * scale
        p = jnp.exp2(s * scale - top)
        total = jnp.sum(p, axis=-1, keepdims=True)
        mixed = jnp.dot(
            p.astype(jnp.bfloat16), v_ref[prompt], preferred_element_type=jnp.float32
        )
        mixed = (mixed / total).astype(jnp.bfloat16)
        hi, mid, lo = three_terms(top)
        lane = lax.broadcasted_iota(jnp.int32, (queries, 128), 1)
        at_row = lax.broadcasted_iota(jnp.int32, (queries, 128), 0) % per_row
        part = lane // per_row
        stat = jnp.where(part == 0, hi, jnp.where(part == 1, mid, jnp.where(part == 2, lo, total)))
        stat = jnp.where(lane % per_row == at_row, stat, 0.0)
        stat = jnp.sum(stat.reshape(BLOCK_ROWS, per_row, 128), axis=1)
        return rows, where, mixed, stat

    def put(rows, where, mixed, stat):
        for j in range(BLOCK_ROWS):
            o, w = where[j]
            out_ref[o, w, :] = mixed[j * per_row : (j + 1) * per_row, :]
            stat_ref[pl.ds(rows[j], 1), :] = stat[j : j + 1, :]

    def clip(b):
        return jnp.minimum(b, blocks - 1)

    def ready(b, waited):
        end = slot_ref[clip(b) * BLOCK_ROWS] % prompts + 1
        lax.fori_loop(waited, end, finish, 0)
        return jnp.maximum(waited, end)

    waited = ready(DEPTH - 1, jnp.int32(0))
    for u in range(DEPTH):
        score(clip(u), u)

    def sweep(i, waited):
        first = i * 2 * DEPTH
        waited = ready(first + 3 * DEPTH - 1, waited)
        for half in range(2):
            here, there = half * DEPTH, (1 - half) * DEPTH
            done = [mix(clip(first + here + u), here + u) for u in range(DEPTH)]
            for u in range(DEPTH):
                score(clip(first + here + DEPTH + u), there + u)
            for d in done:
                put(*d)
        return waited

    waited = lax.fori_loop(0, (blocks + 2 * DEPTH - 1) // (2 * DEPTH), sweep, waited)
    lax.fori_loop(waited, prompts, finish, 0)
    for o in range(owners):
        out_ref[o, body_rows : body_rows + PACK, :] = padded(
            stat_ref[o * OWNER_ROWS : (o + 1) * OWNER_ROWS, :]
        )


def padded(stat):
    pad = jnp.zeros((PACK - OWNER_ROWS, stat.shape[1]), jnp.float32)
    return jnp.concatenate([stat, pad], axis=0).astype(jnp.bfloat16)


def read_stats(per_row, ref_part):
    stat = ref_part.astype(jnp.float32)[:, :OWNER_ROWS, :]
    n = stat.shape[0]
    stat = stat.reshape(n * OWNER_ROWS, 128)
    top = (
        stat + pltpu.roll(stat, 128 - per_row, 1) + pltpu.roll(stat, 128 - 2 * per_row, 1)
    )
    total = pltpu.roll(stat, 128 - 3 * per_row, 1)
    return top.reshape(n, OWNER_ROWS, 128), total.reshape(n, OWNER_ROWS, 128)


def join_kernel(per_row, *refs):
    parts, out_ref = refs[:-1], refs[-1]
    n = len(parts)
    body_rows = OWNER_ROWS * per_row
    lane = lax.broadcasted_iota(jnp.int32, (OWNER_ROWS, 128), 1) // per_row
    for o in range(out_ref.shape[0]):
        stats = [read_stats(per_row, ref[o : o + 1, body_rows : body_rows + PACK, :]) for ref in parts]
        tops = [t[0] for t, _ in stats]
        peak = functools.reduce(jnp.maximum, tops)
        weights = [total[0] * jnp.exp2(t - peak) for t, (_, total) in zip(tops, stats)]
        summed = functools.reduce(jnp.add, weights)
        table = jnp.concatenate([w / summed for w in weights], axis=0)
        table = jnp.transpose(table)[:per_row, :]
        for j in range(OWNER_ROWS):
            span = slice(j * per_row, (j + 1) * per_row)
            acc = jnp.zeros((per_row, 128), jnp.float32)
            for i in range(n):
                at = i * OWNER_ROWS + j
                acc += table[:, at : at + 1] * parts[i][o, span, :].astype(jnp.float32)
            out_ref[o, span, :] = acc.astype(jnp.bfloat16)
        hi, mid, lo = three_terms(peak)
        stat = jnp.where(
            lane == 0,
            hi,
            jnp.where(
                lane == 1,
                pltpu.roll(mid, per_row, 1),
                jnp.where(
                    lane == 2, pltpu.roll(lo, 2 * per_row, 1), pltpu.roll(summed, 3 * per_row, 1)
                ),
            ),
        )
        out_ref[o, body_rows : body_rows + PACK, :] = padded(stat)


def own_kernel(per_row, steps, scale, len_ref, q_ref, kv_ref, fresh_ref, out_ref, top_ref, total_ref):
    rows, length = kv_ref.shape[1], kv_ref.shape[2]
    group = per_row // steps
    pos = lax.broadcasted_iota(jnp.int32, (per_row, length), 1)
    step_of = lax.broadcasted_iota(jnp.int32, (per_row, PACK), 0) // group
    fresh_at = lax.broadcasted_iota(jnp.int32, (per_row, PACK), 1)
    over_last = (((1,), (1,)), ((), ()))
    for j in range(rows):
        part = pl.ds(j * per_row, per_row)
        q = q_ref[part, :]
        s = lax.dot_general(q, kv_ref[0, j], over_last, preferred_element_type=jnp.float32)
        s = jnp.where(pos < len_ref[j], s * scale, -jnp.inf)
        f = lax.dot_general(q, fresh_ref[0, j], over_last, preferred_element_type=jnp.float32)
        f = jnp.where(fresh_at <= step_of, f * scale, -jnp.inf)
        top = jnp.maximum(
            jnp.max(s, axis=-1, keepdims=True), jnp.max(f, axis=-1, keepdims=True)
        )
        ps, pf = jnp.exp2(s - top), jnp.exp2(f - top)
        total = jnp.sum(ps, axis=-1, keepdims=True) + jnp.sum(pf, axis=-1, keepdims=True)
        mixed = jnp.dot(ps.astype(jnp.bfloat16), kv_ref[1, j], preferred_element_type=jnp.float32)
        mixed += jnp.dot(
            pf.astype(jnp.bfloat16), fresh_ref[1, j], preferred_element_type=jnp.float32
        )
        out_ref[part, :] = mixed
        top_ref[part, :] = jnp.broadcast_to(top, (per_row, 128))
        total_ref[part, :] = jnp.broadcast_to(total, (per_row, 128))


def project_kernel(chip_ref, *refs):
    tokens_ref, weights, out_ref = refs[0], refs[1:-1], refs[-1]
    slots = out_ref.shape[0]
    for t, weight in enumerate(weights):
        out_ref[(chip_ref[0] + slots - t) % slots] = jnp.dot(
            tokens_ref[...], weight[...], preferred_element_type=jnp.float32
        ).astype(jnp.bfloat16)


def merge_kernel(per_row, parts_ref, own_ref, top_ref, total_ref, out_ref):
    sources = parts_ref.shape[0]
    rows = OWNER_ROWS
    top, total = read_stats(per_row, parts_ref[:, rows * per_row : rows * per_row + PACK, :])
    peak = jnp.max(top, axis=0)
    weight = total * jnp.exp2(top - peak[None])
    summed = jnp.sum(weight, axis=0)
    for j in range(rows):
        table = jnp.concatenate(
            [weight[:, j, :], peak[j : j + 1, :], summed[j : j + 1, :], jnp.zeros((6, 128), jnp.float32)],
            axis=0,
        )
        table = jnp.transpose(table)[:per_row, :]
        span = slice(j * per_row, (j + 1) * per_row)
        acc = jnp.zeros((per_row, 128), jnp.float32)
        for i in range(sources):
            acc += table[:, i : i + 1] * parts_ref[i, span, :].astype(jnp.float32)
        prompt_top = table[:, sources : sources + 1]
        prompt_sum = table[:, sources + 1 : sources + 2]
        own_top = top_ref[span, :]
        best = jnp.maximum(prompt_top, own_top)
        a, b = jnp.exp2(prompt_top - best), jnp.exp2(own_top - best)
        num = acc * a + own_ref[span, :] * b
        den = prompt_sum * a + total_ref[span, :] * b
        out_ref[span, :] = (num / den).astype(jnp.bfloat16)


def spread(x, groups):
    n = len(groups[0])
    return lax.all_to_all(
        jnp.broadcast_to(x[None], (n,) + x.shape), "seq", 0, 0, axis_index_groups=groups
    )


def shift_x(x, by):
    pairs = [
        (i * SEQ_Z + z, (i + by) % SEQ_X * SEQ_Z + z) for i in range(SEQ_X) for z in range(SEQ_Z)
    ]
    return lax.ppermute(x, "seq", pairs)


def shards(
    queries,
    new_kv,
    prompt_keys,
    prompt_values,
    suffix_kv,
    prompt_ids,
    suffix_lengths,
    token_ids,
    embedding,
    out_weight,
):
    steps, rows_own, heads_own, head_dim = queries.shape
    prompts, positions = prompt_keys.shape[0], prompt_keys.shape[1]
    per_row = steps * heads_own
    scale = head_dim ** (-0.5) * LOG2E
    own_q = jnp.transpose(queries, (1, 0, 2, 3)).reshape(rows_own * per_row, head_dim)
    ids = jnp.pad(
        prompt_ids.reshape(1, rows_own).astype(jnp.bfloat16),
        ((0, PACK - 1), (0, head_dim - rows_own)),
    )
    packed = jnp.concatenate([own_q, ids])
    row_q = spread(packed, Z_GROUPS)
    owners = row_q.shape[0]
    chunk_rows = owners * rows_own
    blocks = chunk_rows // BLOCK_ROWS + prompts
    payload = jax.ShapeDtypeStruct(row_q.shape, jnp.bfloat16)
    keys = in_hbm(prompt_keys.reshape(prompts, positions, head_dim))
    values = in_hbm(prompt_values.reshape(prompts, positions, head_dim))
    pairs = chunk_rows * per_row * positions
    attend = pl.pallas_call(
        functools.partial(prompt_kernel, per_row, scale),
        out_shape=payload,
        in_specs=[VMEM, HBM, HBM],
        out_specs=VMEM,
        scratch_shapes=[
            pltpu.VMEM(keys.shape, jnp.bfloat16),
            pltpu.VMEM(values.shape, jnp.bfloat16),
            pltpu.VMEM((chunk_rows, 128), jnp.float32),
            pltpu.VMEM((2 * DEPTH, BLOCK_ROWS * per_row, positions), jnp.float32),
            pltpu.SMEM((blocks * BLOCK_ROWS,), jnp.int32),
            pltpu.SMEM((prompts,), jnp.int32),
            pltpu.VMEM((owners, 128), jnp.int32),
            pltpu.SMEM((owners, 128), jnp.int32),
            pltpu.SemaphoreType.DMA(()),
            pltpu.SemaphoreType.DMA((prompts,)),
            pltpu.SemaphoreType.DMA((prompts,)),
        ],
        compiler_params=pltpu.CompilerParams(vmem_limit_bytes=24 << 20),
        cost_estimate=pl.CostEstimate(
            flops=8 * pairs * head_dim, bytes_accessed=4 << 20, transcendentals=pairs
        ),
        name="prompt",
    )

    def partial_of(q):
        return attend(q, keys, values)

    turns = [1, SEQ_X - 1, 2]
    arrived = [shift_x(row_q, t) for t in turns]
    first, arrived[0] = lax.optimization_barrier((partial_of(row_q), arrived[0]))
    partials = [first]
    partials += [shift_x(partial_of(q), -t) for q, t in zip(arrived, turns)]
    joined = pl.pallas_call(
        functools.partial(join_kernel, per_row),
        out_shape=payload,
        in_specs=[VMEM] * len(partials),
        out_specs=VMEM,
        compiler_params=pltpu.CompilerParams(vmem_limit_bytes=32 << 20),
        name="join",
    )(*partials)
    fresh = jnp.transpose(new_kv[:, :, :, 0, :], (0, 2, 1, 3))
    fresh = jnp.pad(fresh, ((0, 0), (0, 0), (0, PACK - steps), (0, 0)))
    wide = jax.ShapeDtypeStruct((rows_own * per_row, head_dim), jnp.float32)
    own = pl.pallas_call(
        functools.partial(own_kernel, per_row, steps, scale),
        out_shape=[wide, wide, wide],
        in_specs=[SMEM, VMEM, VMEM, VMEM],
        out_specs=[VMEM] * 3,
        compiler_params=pltpu.CompilerParams(vmem_limit_bytes=32 << 20),
        name="own",
    )(suffix_lengths, own_q, suffix_kv[:, :, :, 0, :], fresh)

    joined, weight = lax.optimization_barrier((joined, out_weight))
    near = [shift_x(weight, 1), shift_x(weight, 3)]
    received = lax.all_to_all(joined, "seq", 0, 0, axis_index_groups=Z_GROUPS)
    vocab_own = embedding.shape[0]
    local_ids = token_ids.reshape(-1) - lax.axis_index("head") * vocab_own
    inside = (local_ids >= 0) & (local_ids < vocab_own)
    embedded = jnp.take(embedding, jnp.clip(local_ids, 0, vocab_own - 1), axis=0)
    embedded = jnp.where(inside[:, None], embedded, jnp.zeros_like(embedded))
    received, embedded, *near = lax.optimization_barrier((received, embedded, *near))
    attention = pl.pallas_call(
        functools.partial(merge_kernel, per_row),
        out_shape=jax.ShapeDtypeStruct((rows_own * per_row, head_dim), jnp.bfloat16),
        in_specs=[VMEM] * 4,
        out_specs=VMEM,
        compiler_params=pltpu.CompilerParams(vmem_limit_bytes=32 << 20),
        name="merge",
    )(received, *own)
    attention = attention.reshape(rows_own * steps, heads_own * head_dim)
    attention, weight = lax.optimization_barrier((attention, weight))
    weights_x = [weight, near[0], shift_x(weight, 2), near[1]]
    attention_z = spread(attention, Z_GROUPS).reshape(-1, heads_own * head_dim)

    heads = lax.axis_size("head")
    chip = (lax.axis_index("seq") // SEQ_Z).astype(jnp.int32).reshape(1)
    projected = pl.pallas_call(
        project_kernel,
        out_shape=jax.ShapeDtypeStruct(
            (SEQ_X, attention_z.shape[0], out_weight.shape[1]), jnp.bfloat16
        ),
        in_specs=[SMEM] + [VMEM] * (1 + len(weights_x)),
        out_specs=VMEM,
        compiler_params=pltpu.CompilerParams(vmem_limit_bytes=24 << 20),
        name="project",
    )(chip, attention_z, *weights_x)
    projected = lax.all_to_all(projected, "seq", 0, 0, axis_index_groups=X_GROUPS)
    projected = projected.reshape(embedded.shape).astype(jnp.float32)
    terms = (projected + embedded.astype(jnp.float32)).astype(jnp.bfloat16)
    terms = lax.all_to_all(terms.reshape(heads, -1, terms.shape[1]), "head", 0, 0)
    hidden = jnp.sum(terms.astype(jnp.float32), axis=0).astype(jnp.bfloat16)
    return hidden.reshape(-1, steps, hidden.shape[1])


def solution(mesh):
    return jax.shard_map(
        shards,
        mesh=mesh,
        in_specs=(
            P(None, "seq", "head", None),
            P(None, None, "seq", "head", None),
            P(None, "seq", "head", None),
            P(None, "seq", "head", None),
            P(None, "seq", None, "head", None),
            P("seq", None),
            P("seq"),
            P(),
            P("head", "seq"),
            P("head", "seq"),
        ),
        out_specs=P("head", None, "seq"),
        check_vma=False,
    )
```

```python
import functools
import math

import jax
import jax.numpy as jnp
from jax import lax
from jax.experimental import pallas as pl
from jax.experimental.pallas import tpu as pltpu
from jax.sharding import PartitionSpec as P

BLOCK_ROWS = 4
DEPTH = 2
OWNER_ROWS = 8
PACK = 16
LOG2E = 1.0 / math.log(2.0)
SEQ_X, SEQ_Z = 4, 8
Z_GROUPS = [[x * SEQ_Z + z for z in range(SEQ_Z)] for x in range(SEQ_X)]
X_GROUPS = [[x * SEQ_Z + z for x in range(SEQ_X)] for z in range(SEQ_Z)]
VMEM = pl.BlockSpec(memory_space=pltpu.VMEM)
SMEM = pl.BlockSpec(memory_space=pltpu.SMEM)
HBM = pl.BlockSpec(memory_space=pltpu.HBM)


def three_terms(x):
    hi = x.astype(jnp.bfloat16).astype(jnp.float32)
    mid = (x - hi).astype(jnp.bfloat16).astype(jnp.float32)
    return hi, mid, (x - hi) - mid


def in_hbm(x):
    return pltpu.with_memory_space_constraint(x, pltpu.HBM)


def slot_table(rows, prompts, ids_ref, slot_ref, next_ref):
    for p in range(prompts):
        next_ref[p] = 0

    def count(r, carry):
        p = ids_ref[r // OWNER_ROWS, r % OWNER_ROWS]
        next_ref[p] = next_ref[p] + 1
        return carry

    def place(r, carry):
        p = ids_ref[r // OWNER_ROWS, r % OWNER_ROWS]
        k = next_ref[p]
        slot_ref[k] = r * prompts + p
        next_ref[p] = k + 1
        return carry

    lax.fori_loop(0, rows, count, 0, unroll=True)
    end = jnp.int32(0)
    ends = []
    for p in range(prompts):
        need = (next_ref[p] + BLOCK_ROWS - 1) // BLOCK_ROWS * BLOCK_ROWS
        next_ref[p] = end
        end = end + need
        ends.append(end)
    lax.fori_loop(0, rows, place, 0, unroll=True)
    for p in range(prompts):
        filled = next_ref[p]
        last = slot_ref[jnp.maximum(filled - 1, 0)]
        for i in range(BLOCK_ROWS - 1):

            @pl.when(filled + i < ends[p])
            def _():
                slot_ref[filled + i] = last

    return end // BLOCK_ROWS


def prompt_kernel(
    per_row,
    scale,
    q_ref,
    k_hbm,
    v_hbm,
    out_ref,
    k_ref,
    v_ref,
    stat_ref,
    score_ref,
    slot_ref,
    next_ref,
    held_ref,
    ids_ref,
    ids_sem,
    k_sem,
    v_sem,
):
    owners = out_ref.shape[0]
    prompts = k_ref.shape[0]
    queries = BLOCK_ROWS * per_row
    body_rows = OWNER_ROWS * per_row
    def load(p):
        return (
            pltpu.make_async_copy(k_hbm.at[p], k_ref.at[p], k_sem.at[p]),
            pltpu.make_async_copy(v_hbm.at[p], v_ref.at[p, :, :128], v_sem.at[p]),
        )

    def finish(p, carry):
        for copy in load(p):
            copy.wait()
        return carry

    held_ref[...] = q_ref[:, body_rows, :].astype(jnp.float32).astype(jnp.int32)
    ids_copy = pltpu.make_async_copy(held_ref, ids_ref, ids_sem)
    ids_copy.start()
    for p in range(prompts):
        for copy in load(p):
            copy.start()
    for p in range(prompts):
        v_ref[p, :, 128:] = jnp.ones((v_ref.shape[1], 128), jnp.bfloat16)
    ids_copy.wait()
    blocks = slot_table(owners * OWNER_ROWS, prompts, ids_ref, slot_ref, next_ref)

    def locate(b):
        codes = [slot_ref[b * BLOCK_ROWS + j] for j in range(BLOCK_ROWS)]
        rows = [code // prompts for code in codes]
        where = [
            (r // OWNER_ROWS, pl.ds(pl.multiple_of(r % OWNER_ROWS * per_row, per_row), per_row))
            for r in rows
        ]
        return rows, where, codes[0] % prompts

    def score(b, at):
        _, where, prompt = locate(b)
        q = jnp.concatenate([q_ref[o, w, :] for o, w in where], axis=0)
        score_ref[at] = scale * lax.dot_general(
            q, k_ref[prompt], (((1,), (1,)), ((), ())), preferred_element_type=jnp.float32
        )

    def mix(b, at):
        rows, where, prompt = locate(b)
        s = score_ref[at]
        top = jnp.max(s, axis=-1, keepdims=True)
        p = jnp.exp2(s - top)
        mixed = jnp.dot(
            p.astype(jnp.bfloat16), v_ref[prompt], preferred_element_type=jnp.float32
        )
        total = mixed[:, 128:]
        mixed = (mixed[:, :128] / total).astype(jnp.bfloat16)
        hi, mid, lo = three_terms(top)
        lane = lax.broadcasted_iota(jnp.int32, (queries, 128), 1)
        at_row = lax.broadcasted_iota(jnp.int32, (queries, 128), 0) % per_row
        part = lane // per_row
        stat = jnp.where(part == 0, hi, jnp.where(part == 1, mid, jnp.where(part == 2, lo, total)))
        stat = jnp.where(lane % per_row == at_row, stat, 0.0)
        stat = jnp.sum(stat.reshape(BLOCK_ROWS, per_row, 128), axis=1)
        return rows, where, mixed, stat

    def put(rows, where, mixed, stat):
        for j in range(BLOCK_ROWS):
            o, w = where[j]
            out_ref[o, w, :] = mixed[j * per_row : (j + 1) * per_row, :]
            stat_ref[pl.ds(rows[j], 1), :] = stat[j : j + 1, :]

    def clip(b):
        return jnp.minimum(b, blocks - 1)

    def ready(b, waited):
        end = slot_ref[clip(b) * BLOCK_ROWS] % prompts + 1
        lax.fori_loop(waited, end, finish, 0)
        return jnp.maximum(waited, end)

    waited = ready(DEPTH - 1, jnp.int32(0))
    for u in range(DEPTH):
        score(clip(u), u)

    def sweep(i, waited):
        first = i * 2 * DEPTH
        waited = ready(first + 3 * DEPTH - 1, waited)
        for half in range(2):
            here, there = half * DEPTH, (1 - half) * DEPTH
            done = [mix(clip(first + here + u), here + u) for u in range(DEPTH)]
            for u in range(DEPTH):
                score(clip(first + here + DEPTH + u), there + u)
            for d in done:
                put(*d)
        return waited

    waited = lax.fori_loop(0, (blocks + 2 * DEPTH - 1) // (2 * DEPTH), sweep, waited)
    lax.fori_loop(waited, prompts, finish, 0)
    for o in range(owners):
        out_ref[o, body_rows : body_rows + PACK, :] = padded(
            stat_ref[o * OWNER_ROWS : (o + 1) * OWNER_ROWS, :]
        )


def padded(stat):
    pad = jnp.zeros((PACK - OWNER_ROWS, stat.shape[1]), jnp.float32)
    return jnp.concatenate([stat, pad], axis=0).astype(jnp.bfloat16)


def read_stats(per_row, ref_part):
    stat = ref_part.astype(jnp.float32)[:, :OWNER_ROWS, :]
    n = stat.shape[0]
    stat = stat.reshape(n * OWNER_ROWS, 128)
    top = (
        stat + pltpu.roll(stat, 128 - per_row, 1) + pltpu.roll(stat, 128 - 2 * per_row, 1)
    )
    total = pltpu.roll(stat, 128 - 3 * per_row, 1)
    return top.reshape(n, OWNER_ROWS, 128), total.reshape(n, OWNER_ROWS, 128)


def join_kernel(per_row, *refs):
    parts, out_ref = refs[:-1], refs[-1]
    n = len(parts)
    body_rows = OWNER_ROWS * per_row
    lane = lax.broadcasted_iota(jnp.int32, (OWNER_ROWS, 128), 1) // per_row
    query = lax.broadcasted_iota(jnp.int32, (per_row, 128), 1) % per_row
    diagonal = query == lax.broadcasted_iota(jnp.int32, (per_row, 128), 0)
    for o in range(out_ref.shape[0]):
        stats = [read_stats(per_row, ref[o : o + 1, body_rows : body_rows + PACK, :]) for ref in parts]
        tops = [t[0] for t, _ in stats]
        peak = functools.reduce(jnp.maximum, tops)
        weights = [total[0] * jnp.exp2(t - peak) for t, (_, total) in zip(tops, stats)]
        summed = functools.reduce(jnp.add, weights)
        share = weights[-1] / summed
        for i in reversed(range(n)):
            placed = pltpu.roll(weights[i] / summed, i * per_row, 1) if i else weights[i] / summed
            share = jnp.where(lane == i, placed, share)
        high = share.astype(jnp.bfloat16).astype(jnp.float32)
        low = share - high
        for j in range(OWNER_ROWS):
            span = slice(j * per_row, (j + 1) * per_row)
            stacked = jnp.concatenate([part[o, span, :] for part in parts], axis=0)
            acc = jnp.zeros((per_row, 128), jnp.float32)
            for piece in (high, low):
                rows = jnp.broadcast_to(piece[j : j + 1, :], (per_row, 128))
                acc += jnp.dot(
                    jnp.where(diagonal, rows, 0.0).astype(jnp.bfloat16),
                    stacked,
                    preferred_element_type=jnp.float32,
                )
            out_ref[o, span, :] = acc.astype(jnp.bfloat16)
        hi, mid, lo = three_terms(peak)
        stat = jnp.where(
            lane == 0,
            hi,
            jnp.where(
                lane == 1,
                pltpu.roll(mid, per_row, 1),
                jnp.where(
                    lane == 2, pltpu.roll(lo, 2 * per_row, 1), pltpu.roll(summed, 3 * per_row, 1)
                ),
            ),
        )
        out_ref[o, body_rows : body_rows + PACK, :] = padded(stat)


def own_kernel(per_row, steps, scale, len_ref, q_ref, kv_ref, fresh_ref, out_ref, top_ref, total_ref):
    rows, length = kv_ref.shape[1], kv_ref.shape[2]
    group = per_row // steps
    pos = lax.broadcasted_iota(jnp.int32, (per_row, length), 1)
    step_of = lax.broadcasted_iota(jnp.int32, (per_row, PACK), 0) // group
    fresh_at = lax.broadcasted_iota(jnp.int32, (per_row, PACK), 1)
    over_last = (((1,), (1,)), ((), ()))
    for j in range(rows):
        part = pl.ds(j * per_row, per_row)
        q = q_ref[part, :]
        s = lax.dot_general(q, kv_ref[0, j], over_last, preferred_element_type=jnp.float32)
        s = jnp.where(pos < len_ref[j], s * scale, -jnp.inf)
        f = lax.dot_general(q, fresh_ref[0, j], over_last, preferred_element_type=jnp.float32)
        f = jnp.where(fresh_at <= step_of, f * scale, -jnp.inf)
        top = jnp.maximum(
            jnp.max(s, axis=-1, keepdims=True), jnp.max(f, axis=-1, keepdims=True)
        )
        ps, pf = jnp.exp2(s - top), jnp.exp2(f - top)
        total = jnp.sum(ps, axis=-1, keepdims=True) + jnp.sum(pf, axis=-1, keepdims=True)
        mixed = jnp.dot(ps.astype(jnp.bfloat16), kv_ref[1, j], preferred_element_type=jnp.float32)
        mixed += jnp.dot(
            pf.astype(jnp.bfloat16), fresh_ref[1, j], preferred_element_type=jnp.float32
        )
        out_ref[part, :] = mixed
        top_ref[part, :] = jnp.broadcast_to(top, (per_row, 128))
        total_ref[part, :] = jnp.broadcast_to(total, (per_row, 128))


def project_kernel(chip_ref, *refs):
    tokens_ref, weights, out_ref = refs[0], refs[1:-1], refs[-1]
    slots = out_ref.shape[0]
    for t, weight in enumerate(weights):
        out_ref[(chip_ref[0] + slots - t) % slots] = jnp.dot(
            tokens_ref[...], weight[...], preferred_element_type=jnp.float32
        ).astype(jnp.bfloat16)


def merge_kernel(per_row, parts_ref, own_ref, top_ref, total_ref, out_ref):
    sources = parts_ref.shape[0]
    rows = OWNER_ROWS
    top, total = read_stats(per_row, parts_ref[:, rows * per_row : rows * per_row + PACK, :])
    peak = jnp.max(top, axis=0)
    weight = total * jnp.exp2(top - peak[None])
    summed = jnp.sum(weight, axis=0)
    for j in range(rows):
        table = jnp.concatenate(
            [weight[:, j, :], peak[j : j + 1, :], summed[j : j + 1, :], jnp.zeros((6, 128), jnp.float32)],
            axis=0,
        )
        table = jnp.transpose(table)[:per_row, :]
        span = slice(j * per_row, (j + 1) * per_row)
        acc = jnp.zeros((per_row, 128), jnp.float32)
        for i in range(sources):
            acc += table[:, i : i + 1] * parts_ref[i, span, :].astype(jnp.float32)
        prompt_top = table[:, sources : sources + 1]
        prompt_sum = table[:, sources + 1 : sources + 2]
        own_top = top_ref[span, :]
        best = jnp.maximum(prompt_top, own_top)
        a, b = jnp.exp2(prompt_top - best), jnp.exp2(own_top - best)
        num = acc * a + own_ref[span, :] * b
        den = prompt_sum * a + total_ref[span, :] * b
        out_ref[span, :] = (num / den).astype(jnp.bfloat16)


def spread(x, groups):
    n = len(groups[0])
    return lax.all_to_all(
        jnp.broadcast_to(x[None], (n,) + x.shape), "seq", 0, 0, axis_index_groups=groups
    )


def shift_x(x, by):
    pairs = [
        (i * SEQ_Z + z, (i + by) % SEQ_X * SEQ_Z + z) for i in range(SEQ_X) for z in range(SEQ_Z)
    ]
    return lax.ppermute(x, "seq", pairs)


def shards(
    queries,
    new_kv,
    prompt_keys,
    prompt_values,
    suffix_kv,
    prompt_ids,
    suffix_lengths,
    token_ids,
    embedding,
    out_weight,
):
    steps, rows_own, heads_own, head_dim = queries.shape
    prompts, positions = prompt_keys.shape[0], prompt_keys.shape[1]
    per_row = steps * heads_own
    scale = head_dim ** (-0.5) * LOG2E
    own_q = jnp.transpose(queries, (1, 0, 2, 3)).reshape(rows_own * per_row, head_dim)
    ids = jnp.pad(
        prompt_ids.reshape(1, rows_own).astype(jnp.bfloat16),
        ((0, PACK - 1), (0, head_dim - rows_own)),
    )
    packed = jnp.concatenate([own_q, ids])
    row_q = spread(packed, Z_GROUPS)
    owners = row_q.shape[0]
    chunk_rows = owners * rows_own
    blocks = chunk_rows // BLOCK_ROWS + prompts
    payload = jax.ShapeDtypeStruct(row_q.shape, jnp.bfloat16)
    keys = in_hbm(prompt_keys.reshape(prompts, positions, head_dim))
    values = in_hbm(prompt_values.reshape(prompts, positions, head_dim))
    pairs = chunk_rows * per_row * positions
    attend = pl.pallas_call(
        functools.partial(prompt_kernel, per_row, scale),
        out_shape=payload,
        in_specs=[VMEM, HBM, HBM],
        out_specs=VMEM,
        scratch_shapes=[
            pltpu.VMEM(keys.shape, jnp.bfloat16),
            pltpu.VMEM((prompts, positions, 2 * head_dim), jnp.bfloat16),
            pltpu.VMEM((chunk_rows, 128), jnp.float32),
            pltpu.VMEM((2 * DEPTH, BLOCK_ROWS * per_row, positions), jnp.float32),
            pltpu.SMEM((blocks * BLOCK_ROWS,), jnp.int32),
            pltpu.SMEM((prompts,), jnp.int32),
            pltpu.VMEM((owners, 128), jnp.int32),
            pltpu.SMEM((owners, 128), jnp.int32),
            pltpu.SemaphoreType.DMA(()),
            pltpu.SemaphoreType.DMA((prompts,)),
            pltpu.SemaphoreType.DMA((prompts,)),
        ],
        compiler_params=pltpu.CompilerParams(vmem_limit_bytes=24 << 20),
        cost_estimate=pl.CostEstimate(
            flops=8 * pairs * head_dim, bytes_accessed=4 << 20, transcendentals=pairs
        ),
        name="prompt",
    )

    def partial_of(q):
        return attend(q, keys, values)

    turns = [1, SEQ_X - 1, 2]
    arrived = [shift_x(row_q, t) for t in turns]
    first, arrived[0] = lax.optimization_barrier((partial_of(row_q), arrived[0]))
    partials = [first]
    partials += [shift_x(partial_of(q), -t) for q, t in zip(arrived, turns)]
    joined = pl.pallas_call(
        functools.partial(join_kernel, per_row),
        out_shape=payload,
        in_specs=[VMEM] * len(partials),
        out_specs=VMEM,
        compiler_params=pltpu.CompilerParams(vmem_limit_bytes=32 << 20),
        name="join",
    )(*partials)
    fresh = jnp.transpose(new_kv[:, :, :, 0, :], (0, 2, 1, 3))
    fresh = jnp.pad(fresh, ((0, 0), (0, 0), (0, PACK - steps), (0, 0)))
    wide = jax.ShapeDtypeStruct((rows_own * per_row, head_dim), jnp.float32)
    own = pl.pallas_call(
        functools.partial(own_kernel, per_row, steps, scale),
        out_shape=[wide, wide, wide],
        in_specs=[SMEM, VMEM, VMEM, VMEM],
        out_specs=[VMEM] * 3,
        compiler_params=pltpu.CompilerParams(vmem_limit_bytes=32 << 20),
        name="own",
    )(suffix_lengths, own_q, suffix_kv[:, :, :, 0, :], fresh)

    joined, weight = lax.optimization_barrier((joined, out_weight))
    near = [shift_x(weight, 1), shift_x(weight, 3)]
    received = lax.all_to_all(joined, "seq", 0, 0, axis_index_groups=Z_GROUPS)
    vocab_own = embedding.shape[0]
    local_ids = token_ids.reshape(-1) - lax.axis_index("head") * vocab_own
    inside = (local_ids >= 0) & (local_ids < vocab_own)
    embedded = jnp.take(embedding, jnp.clip(local_ids, 0, vocab_own - 1), axis=0)
    embedded = jnp.where(inside[:, None], embedded, jnp.zeros_like(embedded))
    received, embedded, *near = lax.optimization_barrier((received, embedded, *near))
    attention = pl.pallas_call(
        functools.partial(merge_kernel, per_row),
        out_shape=jax.ShapeDtypeStruct((rows_own * per_row, head_dim), jnp.bfloat16),
        in_specs=[VMEM] * 4,
        out_specs=VMEM,
        compiler_params=pltpu.CompilerParams(vmem_limit_bytes=32 << 20),
        name="merge",
    )(received, *own)
    attention = attention.reshape(rows_own * steps, heads_own * head_dim)
    attention, weight = lax.optimization_barrier((attention, weight))
    weights_x = [weight, near[0], shift_x(weight, 2), near[1]]
    attention_z = spread(attention, Z_GROUPS).reshape(-1, heads_own * head_dim)

    heads = lax.axis_size("head")
    chip = (lax.axis_index("seq") // SEQ_Z).astype(jnp.int32).reshape(1)
    projected = pl.pallas_call(
        project_kernel,
        out_shape=jax.ShapeDtypeStruct(
            (SEQ_X, attention_z.shape[0], out_weight.shape[1]), jnp.bfloat16
        ),
        in_specs=[SMEM] + [VMEM] * (1 + len(weights_x)),
        out_specs=VMEM,
        compiler_params=pltpu.CompilerParams(vmem_limit_bytes=24 << 20),
        name="project",
    )(chip, attention_z, *weights_x)
    projected = lax.all_to_all(projected, "seq", 0, 0, axis_index_groups=X_GROUPS)
    projected = projected.reshape(embedded.shape).astype(jnp.float32)
    terms = (projected + embedded.astype(jnp.float32)).astype(jnp.bfloat16)
    terms = lax.all_to_all(terms.reshape(heads, -1, terms.shape[1]), "head", 0, 0)
    hidden = jnp.sum(terms.astype(jnp.float32), axis=0).astype(jnp.bfloat16)
    return hidden.reshape(-1, steps, hidden.shape[1])


def solution(mesh):
    return jax.shard_map(
        shards,
        mesh=mesh,
        in_specs=(
            P(None, "seq", "head", None),
            P(None, None, "seq", "head", None),
            P(None, "seq", "head", None),
            P(None, "seq", "head", None),
            P(None, "seq", None, "head", None),
            P("seq", None),
            P("seq"),
            P(),
            P("head", "seq"),
            P("head", "seq"),
        ),
        out_specs=P("head", None, "seq"),
        check_vma=False,
    )
```
